1024 devices in a mesh: section: 16 (over y_lo, x, core), expert: 64 (over y_hi, z).
Axes of the slice: x: 4, y: 4 (y_hi: 2, y_lo: 2; y = y_hi * 2 + y_lo), z: 32, core: 2. Of those that a mesh axis runs over, the one named last changes fastest.
Arguments:
- tokens: bfloat16 [2, 16, 4096, 2048], P(None, 'section', 'expert'), may hold values from -24 to 24
- norm_gain: float32 [2048], replicated, may hold values from 0.1 to 1.9
- expert_ids: int32 [2, 16, 4096, 2], P(None, 'section', 'expert'), may hold values from 0 to 23, all different within a row; in each aligned block of 64 rows (0 to 63, 64 to 127, ..., all dimensions but the last counted through in order) at most 6 rows name the same one
- route_scores: float32 [2, 16, 4096, 2], P(None, 'section', 'expert'), may hold values from 0.1 to 1
- placement: int32 [64], replicated, may hold values from 0 to 23, as said below
- w_gate: bfloat16 [64, 2048, 768], P('expert'), as said below
- w_up: bfloat16 [64, 2048, 768], P('expert'), as said below
- w_down: bfloat16 [64, 768, 2048], P('expert'), as said below
Outputs:
- onward: bfloat16 [2, 16, 4096, 2048], P(None, 'section', 'expert')
The draws below stay inside these ranges and needn't reach their ends.
Inputs may be any that keep to these rules, and one draw needn't show every extreme that they name: `expert_ids`: in each micro-batch and section, the 64 rows of one device name each expert at most 6 times, a bound that some block reaches. `placement`: every expert holds two or more slots. `w_gate`: slots with equal placement hold equal gate projections. `w_up`: slots with equal placement hold equal up projections. `w_down`: slots with equal placement hold equal down projections.
All inputs are finite; a program needn't handle non-finite values.
Results may differ from the reference program's by a relative error of at most 0.0039.
Values may be sent and summed in bfloat16 or wider, within the bound.
No kernel may reach another device: no remote copies, remote signals or barrier semaphores. Data moves between devices by JAX's collectives and lax.ppermute only.
A program may use at most 64 MiB of HBM per device.

```python
import math
import jax
import jax.numpy as jnp
import numpy as np
from jax import lax

D = 2048
FF = 768
TOP = 2
MB = 2
TOK = 64
SECTIONS = 16
TOKENS = 4096
SLOTS = 64
EXPERTS = 24
MOST = 6
N_EXPERT = 64


def slot_experts(key):
    owners = jnp.arange(EXPERTS, dtype=jnp.int32)
    extra = jax.random.randint(jax.random.fold_in(key, 101), (SLOTS - 2 * EXPERTS,), 0, EXPERTS, dtype=jnp.int32)
    table = jnp.concatenate([owners, owners, extra])
    shuffle = jax.random.permutation(jax.random.fold_in(key, 102), SLOTS)
    return table[shuffle].astype(jnp.int32)


def expert_table(key, salt, fan_rows, fan_cols):
    owners = slot_experts(key)
    base = jax.random.normal(jax.random.fold_in(key, salt), (EXPERTS, fan_rows, fan_cols), jnp.float32) * fan_rows ** (-0.5)
    return base[owners].astype(jnp.bfloat16)


def draw_placement(key, part):
    return slot_experts(key)


def draw_w_gate(key, part):
    return expert_table(key, 201, D, FF)


def draw_w_up(key, part):
    return expert_table(key, 202, D, FF)


def draw_w_down(key, part):
    return expert_table(key, 203, FF, D)


def draw_tokens(key, part):
    shape = (MB, SECTIONS, TOKENS, D)
    noise = jnp.clip(jax.random.normal(jax.random.fold_in(key, 302), shape, jnp.float32), -4.0, 4.0)
    columns = jnp.exp(jax.random.uniform(jax.random.fold_in(key, 303), (D,), jnp.float32, math.log(0.3), math.log(3.0)))
    row_scale = jnp.exp(jax.random.uniform(jax.random.fold_in(key, 304), (MB, SECTIONS, TOKENS, 1), jnp.float32, math.log(0.5), math.log(2.0)))
    return (noise * columns * row_scale).astype(jnp.bfloat16)


def block_levels(key, dims, shards, smallest, high):
    loudness = 1.0
    for dim, blocks in shards:
        draws = jax.random.uniform(jax.random.fold_in(jax.random.fold_in(key, 6), dim), (blocks,), jnp.float32, smallest / len(shards), high / len(shards))
        loudness = loudness * jnp.repeat(jnp.exp(draws), dims[dim] // blocks).reshape((-1,) + (1,) * (len(dims) - 1 - dim))
    return loudness


def shared_out(stream_key, own, number, rows, number_of, top, limit, lean):
    ranking = jax.random.permutation(stream_key, number_of)
    packed, ordinary = load_shares(number_of, rows * top, limit, lean, True), load_shares(number_of, rows * top, limit, lean, False)
    places = jnp.arange(number_of)

    def named(lengths, turn):
        used = int((lengths > 0).sum())
        fixed = max(1, used // 4)
        moved = fixed + (places - fixed + turn * (used - fixed)) % max(1, number_of - fixed)
        return jnp.zeros((number_of,), jnp.int32).at[ranking[jnp.where(places < fixed, places, moved)]].set(jnp.asarray(lengths, jnp.int32))

    lengths = jnp.where(number % 4 == 0, named(packed, number // 4), named(ordinary, number - number // 4 - 1))
    mixed = jax.random.permutation(jax.random.fold_in(own, 3), number_of)
    giver, receiver = mixed[0:number_of // 2 * 2:2], mixed[1:number_of // 2 * 2:2]
    room = jnp.minimum(lengths[giver] - 1, limit - lengths[receiver]) // 2
    room = jnp.where((giver == ranking[0]) | (receiver == ranking[0]) | (lengths[receiver] == 0), 0, jnp.maximum(room, 0))
    moved = jax.random.randint(jax.random.fold_in(own, 4), (number_of // 2,), 0, 1 << 20) % (room + 1)
    lengths = lengths.at[giver].add(-moved).at[receiver].add(moved)
    members = jnp.searchsorted(jnp.cumsum(lengths), jnp.arange(rows * top), side="right").astype(jnp.int32)
    listing = members.reshape(top, rows).T
    listing = listing[jax.random.permutation(jax.random.fold_in(own, 1), rows)]
    turn = jax.random.randint(jax.random.fold_in(own, 2), (rows, 1), 0, top)
    return jnp.take_along_axis(listing, (jnp.arange(top)[None, :] + turn) % top, axis=1)


def load_shares(count, total, reach, lean, full):
    loads = [(1 << 20) // math.isqrt(grade ** lean) + 1 for grade in range(1, count + 1)]
    largest = reach if full else min(reach, max(-(-total // count), total * loads[0] // sum(loads)))
    least = 1 if total - largest >= count - 1 else 0
    given, spare = [largest] + [least] * (count - 1), total - largest - least * (count - 1)
    while spare > 0:
        candidates = [i for i in range(1, count) if given[i] < largest] or [i for i in range(1, count) if given[i] < reach]
        pool, remaining = sum([loads[i] for i in candidates]), spare
        for i in candidates:
            more = min(reach - given[i], max(1, remaining * loads[i] // pool), spare)
            given[i] = given[i] + more
            spare = spare - more
    return np.array(given)


def setup_inputs(seed: int = 0) -> dict:
    splits = jax.random.split(jax.random.key(seed), 9)
    tokens = draw_tokens(jax.random.fold_in(splits[8], 71), 0)
    norm_gain = jnp.clip(1.0 + 0.18 * jax.random.normal(splits[1], (D,), jnp.float32), 0.1, 1.9)
    expert_ids_keys = jax.random.split(jax.random.fold_in(splits[2], 1), MB * SECTIONS * TOKENS // TOK)
    expert_ids_turns = jax.random.permutation(jax.random.fold_in(splits[2], 3), MB * SECTIONS * TOKENS // TOK)
    expert_ids = jax.vmap(lambda own, number: shared_out(jax.random.fold_in(splits[2], 2), own, number, TOK, EXPERTS, TOP, MOST, 2))(expert_ids_keys, expert_ids_turns).reshape((MB, SECTIONS, TOKENS, TOP))
    route_scores = jnp.clip(jnp.exp(math.log(1.0) - 2.3025851 * jax.random.uniform(splits[3], (MB, SECTIONS, TOKENS, TOP), jnp.float32) ** block_levels(splits[3], (MB, SECTIONS, TOKENS, TOP), ((1, 16), (2, 64)), -0.2, 0.2)), 0.1, 1.0)
    placement = draw_placement(jax.random.fold_in(splits[8], 71), 0)
    w_gate = draw_w_gate(jax.random.fold_in(splits[8], 71), 0)
    w_up = draw_w_up(jax.random.fold_in(splits[8], 71), 0)
    w_down = draw_w_down(jax.random.fold_in(splits[8], 71), 0)
    return dict(tokens=tokens, norm_gain=norm_gain, expert_ids=expert_ids, route_scores=route_scores, placement=placement, w_gate=w_gate, w_up=w_up, w_down=w_down)


EPSILON = 1e-06

def reference(tokens, norm_gain, expert_ids, route_scores, placement, w_gate, w_up, w_down):
    expert_range = jnp.arange(EXPERTS, dtype=jnp.int32)
    slot_range = jnp.arange(SLOTS, dtype=jnp.int32)
    first_slot = lax.optimization_barrier(jnp.min(jnp.where(placement[None, :] == expert_range[:, None], slot_range[None, :], SLOTS), axis=1)).astype(jnp.int32)
    capacity = N_EXPERT * MOST
    routed = TOKENS * TOP
    lane = jnp.arange(capacity, dtype=jnp.int32)

    def one_block(block):
        rows, chosen, scores = block
        values = rows.astype(jnp.float32)
        scale = lax.rsqrt(lax.optimization_barrier(jnp.mean(values * values, axis=-1, keepdims=True)) + EPSILON)
        normed = (values * scale * norm_gain.astype(jnp.float32)).astype(jnp.bfloat16)
        probs = scores / lax.optimization_barrier(jnp.sum(scores, axis=1, keepdims=True))
        flat_ids = chosen.reshape(-1).astype(jnp.int32)
        order = jnp.argsort(flat_ids, stable=True).astype(jnp.int32)
        counts = lax.optimization_barrier(jnp.sum((flat_ids[:, None] == expert_range[None, :]).astype(jnp.int32), axis=0))
        starts = (jnp.cumsum(counts) - counts).astype(jnp.int32)

        def one_expert(expert):
            lookup = jnp.clip(starts[expert] + lane, 0, routed - 1).astype(jnp.int32)
            index = order[lookup]
            valid = lane < counts[expert]
            inputs = normed[index // TOP]
            slot = first_slot[expert]
            gate = jnp.dot(inputs, w_gate[slot], preferred_element_type=jnp.float32)
            up = jnp.dot(inputs, w_up[slot], preferred_element_type=jnp.float32)
            hidden = (jax.nn.silu(gate) * up).astype(jnp.bfloat16)
            output = jnp.dot(hidden, w_down[slot], preferred_element_type=jnp.float32).astype(jnp.bfloat16)
            kept = jnp.where(valid[:, None], output.astype(jnp.float32), jnp.zeros_like(output, dtype=jnp.float32))
            return (kept, index)
        outputs, indices = lax.map(one_expert, expert_range)
        placed = jnp.zeros((routed, D), jnp.float32).at[indices.reshape(-1)].add(outputs.reshape(-1, D))
        moe = lax.optimization_barrier(jnp.sum(probs[:, :, None] * placed.reshape(TOKENS, TOP, D), axis=1))
        return (values + moe).astype(jnp.bfloat16)
    blocks = lax.map(one_block, (tokens.reshape(MB * SECTIONS, TOKENS, D), expert_ids.reshape(MB * SECTIONS, TOKENS, TOP), route_scores.reshape(MB * SECTIONS, TOKENS, TOP)))
    mixed = blocks.reshape(MB, SECTIONS, TOKENS, D)
    empty = jnp.zeros((1, TOKENS, D), mixed.dtype)
    forward = jnp.concatenate([empty, mixed[0, :-1]], axis=0)
    backward = jnp.concatenate([mixed[1, 1:], empty], axis=0)
    return jnp.stack([forward, backward], axis=0)
```

```python
import jax
import jax.numpy as jnp
from jax import lax
from jax.sharding import PartitionSpec as P

EPSILON = 1e-06


def passed_along(x, axis, by):
    peers = lax.axis_size(axis)
    pairs = [(i, i + by) for i in range(peers) if 0 <= i + by < peers]
    return lax.ppermute(x, axis, pairs)


def normalize(rows, gain):
    values = rows.astype(jnp.float32)
    scale = lax.rsqrt(jnp.mean(values * values, axis=-1, keepdims=True) + EPSILON)
    return (values * scale * gain).astype(jnp.bfloat16)


def exclusive_rank(onehot):
    before = jnp.cumsum(onehot, axis=0) - onehot
    return jnp.sum(before * onehot, axis=1)


def route_rows(chosen, placement, experts, capacity):
    flat_ids = chosen.reshape(-1)
    slot_count = placement.shape[0]
    expert_range = jnp.arange(experts, dtype=jnp.int32)
    slot_range = jnp.arange(slot_count, dtype=jnp.int32)
    expert_hit = (flat_ids[:, None] == expert_range[None, :]).astype(jnp.int32)
    owner_hit = (placement[:, None] == expert_range[None, :]).astype(jnp.int32)
    replica_rank = exclusive_rank(owner_hit)
    copies = jnp.sum(owner_hit, axis=0)
    row_copies = jnp.sum(expert_hit * copies[None, :], axis=1)
    wanted = exclusive_rank(expert_hit) % row_copies
    matches = (placement[None, :] == flat_ids[:, None]) & (replica_rank[None, :] == wanted[:, None])
    target = jnp.sum(jnp.where(matches, slot_range[None, :], 0), axis=1)
    target_hit = (target[:, None] == slot_range[None, :]).astype(jnp.int32)
    position = exclusive_rank(target_hit)
    return (target * capacity + position).reshape(chosen.shape)


def body(tokens, norm_gain, expert_ids, route_scores, placement, w_gate, w_up, w_down):
    devices = lax.axis_size("expert")
    slot_count = placement.shape[0]
    experts = slot_count * 3 // 8
    tok_rows = tokens.shape[2]
    width = tokens.shape[3]
    chosen_count = expert_ids.shape[3]
    most_rows = (tok_rows * chosen_count + experts - 1) // experts
    capacity = (most_rows + 1) // 2
    buffer_range = jnp.arange(slot_count * capacity, dtype=jnp.int32)
    sends = []
    mixings = []
    for micro in range(2):
        normed = normalize(tokens[micro, 0], norm_gain)
        flat = route_rows(expert_ids[micro, 0], placement, experts, capacity)
        hits = flat[:, :, None] == buffer_range[None, None, :]
        take = jnp.any(hits, axis=1).astype(jnp.bfloat16)
        send = lax.dot_general(
            take, normed, (((0,), (0,)), ((), ())), preferred_element_type=jnp.float32
        )
        sends.append(send.astype(jnp.bfloat16).reshape(devices, capacity, width))
        scores = route_scores[micro, 0]
        probs = scores / jnp.sum(scores, axis=1, keepdims=True)
        mixings.append(jnp.sum(jnp.where(hits, probs[:, :, None], 0.0), axis=1))
    packed = jnp.stack(sends, axis=1).reshape(devices, -1, 128)
    received = lax.all_to_all(packed, "expert", split_axis=0, concat_axis=0, tiled=True)
    received = received.reshape(-1, width)
    gate = jnp.dot(received, w_gate[0], preferred_element_type=jnp.float32)
    up = jnp.dot(received, w_up[0], preferred_element_type=jnp.float32)
    hidden = (jax.nn.silu(gate) * up).astype(jnp.bfloat16)
    outputs = jnp.dot(hidden, w_down[0], preferred_element_type=jnp.float32).astype(jnp.bfloat16)
    returned = lax.all_to_all(
        outputs.reshape(packed.shape), "expert", split_axis=0, concat_axis=0, tiled=True
    )
    returned = returned.reshape(devices, 2, capacity, width)
    results = []
    for micro in range(2):
        flat_back = returned[:, micro].reshape(-1, width).astype(jnp.float32)
        moe = jnp.dot(
            mixings[micro],
            flat_back,
            precision=lax.Precision.HIGHEST,
            preferred_element_type=jnp.float32,
        )
        results.append((tokens[micro, 0].astype(jnp.float32) + moe).astype(jnp.bfloat16))
    forward = passed_along(results[0], "section", 1)
    backward = passed_along(results[1], "section", -1)
    return jnp.stack([forward, backward], axis=0)[:, None]


def solution(mesh):
    in_specs = (
        P(None, "section", "expert", None),
        P(),
        P(None, "section", "expert", None),
        P(None, "section", "expert", None),
        P(),
        P("expert", None, None),
        P("expert", None, None),
        P("expert", None, None),
    )
    out_specs = P(None, "section", "expert", None)
    return jax.shard_map(body, mesh=mesh, in_specs=in_specs, out_specs=out_specs, check_vma=False)
```

```python
import jax
import jax.numpy as jnp
from jax import lax
from jax.sharding import Mesh
from jax.sharding import PartitionSpec as P

EPSILON = 1e-06
MOST = 6
LANES = 128


def passed_along(x, axis, by):
    peers = lax.axis_size(axis)
    pairs = [(i, i + by) for i in range(peers) if 0 <= i + by < peers]
    return lax.ppermute(x, axis, pairs)


def normalize(rows, gain):
    values = rows.astype(jnp.float32)
    scale = lax.rsqrt(jnp.mean(values * values, axis=-1, keepdims=True) + EPSILON)
    return (values * scale * gain).astype(jnp.bfloat16)


def exclusive_rank(onehot):
    before = jnp.cumsum(onehot, axis=-2) - onehot
    return jnp.sum(before * onehot, axis=-1)


def body(tokens, norm_gain, expert_ids, route_scores, placement, w_gate, w_up, w_down):
    sections = lax.axis_size("section")
    sides = lax.axis_size("side")
    planes = lax.axis_size("plane")
    section = lax.axis_index("section")
    side = lax.axis_index("side")
    plane = lax.axis_index("plane")
    slots = placement.shape[0]
    experts = slots * 3 // 8
    width = tokens.shape[3]
    ff = w_gate.shape[2]
    half_ff = ff // 2
    units = planes // sections
    tok_rows = tokens.shape[2]
    top = expert_ids.shape[3]
    micros = tokens.shape[0]

    expert_range = jnp.arange(experts, dtype=jnp.int32)
    owner = (placement[:, None] == expert_range[None, :]).astype(jnp.int32)
    slot_rank = exclusive_rank(owner)
    slot_range = jnp.arange(slots, dtype=jnp.int32)
    mine = slot_range == side * planes + plane
    half = jnp.sum(jnp.where(mine, slot_rank, 0)) % 2

    k_rows = width // planes
    f_rows = half_ff // units
    blocks = half_ff // LANES

    def piece(number):
        def columns(w):
            part = lax.dynamic_slice(
                w[0], (number * k_rows, half * half_ff), (k_rows, half_ff)
            )
            return part.reshape(k_rows, blocks, LANES).transpose(1, 0, 2)

        down = lax.dynamic_slice(
            w_down[0],
            (half * half_ff + number // sections * f_rows, number % sections * LANES),
            (f_rows, LANES),
        ).reshape(f_rows // k_rows, k_rows, LANES)
        return jnp.concatenate([columns(w_gate), columns(w_up), down], axis=0)

    unit = plane // sections

    def hand_over(flip):
        pairs = []
        for q in range(sections):
            for j in range(planes):
                u = j // sections
                target = q + sections * (1 - u if flip else u)
                pairs.append((q * planes + j, j % sections * planes + target))
        target = section + sections * (1 - unit if flip else unit)
        return lax.ppermute(piece(target), ("section", "plane"), pairs)

    same = hand_over(False)
    other = hand_over(True)
    low = plane < sections
    share = jnp.concatenate(
        [jnp.where(low, same, other), jnp.where(low, other, same)], axis=0
    )
    gathered = lax.all_gather(share, "plane", axis=0)
    weights = gathered.transpose(1, 0, 2, 3)
    per_unit = share.shape[0] // units

    def column_weights(first):
        chosen = [
            weights[u * per_unit + first + b].reshape(width, LANES)
            for u in range(units)
            for b in range(blocks)
        ]
        return jnp.concatenate(chosen, axis=1)

    gate_all = column_weights(0)
    up_all = column_weights(blocks)
    down_all = weights.reshape(units, per_unit, units, sections, k_rows, LANES)[:, 2 * blocks :]
    down_all = down_all.transpose(0, 2, 1, 4, 3, 5).reshape(ff, width)

    per_slot = micros * MOST
    per_host = units * per_slot
    slot_side = slot_range // planes
    slot_plane = slot_range % planes
    slot_base = (
        slot_plane % sections * sides + slot_side
    ) * per_host + slot_plane // sections * per_slot
    bases = [
        jnp.sum(jnp.where(slot_rank == h, slot_base, 0)[:, None] * owner, axis=0) for h in range(2)
    ]
    ids = expert_ids[:, 0].reshape(micros, tok_rows * top)
    hit = (ids[:, :, None] == expert_range).astype(jnp.int32)
    rank = exclusive_rank(hit) + MOST * jnp.arange(micros, dtype=jnp.int32)[:, None]
    scores = route_scores[:, 0]
    probs = scores / jnp.sum(scores, axis=-1, keepdims=True)
    total = sections * sides * per_host
    buffer_range = jnp.arange(total, dtype=jnp.int32)
    take = jnp.zeros((micros * tok_rows, total), jnp.float32)
    mixing = jnp.zeros((micros * tok_rows, total), jnp.float32)
    for base in bases:
        index = (jnp.sum(hit * base, axis=-1) + rank).reshape(micros * tok_rows, top)
        for k in range(top):
            at = index[:, k : k + 1] == buffer_range
            take = jnp.where(at, 1.0, take)
            mixing = jnp.where(at, probs[:, :, k].reshape(-1, 1), mixing)

    normed = normalize(tokens[:, 0].reshape(micros * tok_rows, width), norm_gain)
    send = lax.dot_general(
        take.astype(jnp.bfloat16),
        normed,
        (((0,), (0,)), ((), ())),
        preferred_element_type=jnp.float32,
    ).astype(jnp.bfloat16)
    hosts = sections * sides

    def exchange(x):
        x = x.reshape(hosts, per_host, width)
        x = lax.all_to_all(x, ("section", "side"), split_axis=0, concat_axis=0, tiled=True)
        return x.reshape(total, width)

    received = exchange(send)
    gate = jnp.dot(received, gate_all, preferred_element_type=jnp.float32)
    up = jnp.dot(received, up_all, preferred_element_type=jnp.float32)
    row_unit = jnp.arange(total, dtype=jnp.int32) % per_host // per_slot
    column_unit = jnp.arange(ff, dtype=jnp.int32) // half_ff
    own = row_unit[:, None] == column_unit[None, :]
    hidden = jnp.where(own, jax.nn.silu(gate) * up, 0.0).astype(jnp.bfloat16)
    partial = jnp.dot(hidden, down_all, preferred_element_type=jnp.float32).astype(jnp.bfloat16)
    returned = exchange(partial)
    moe = jnp.dot(
        mixing,
        returned.astype(jnp.float32),
        precision=lax.Precision.HIGHEST,
        preferred_element_type=jnp.float32,
    )
    mixed = tokens[:, 0].astype(jnp.float32) + moe.reshape(micros, tok_rows, width)
    mixed = mixed.astype(jnp.bfloat16)
    forward = passed_along(mixed[0], "section", 1)
    backward = passed_along(mixed[1], "section", -1)
    return jnp.stack([forward, backward], axis=0)[:, None]


def solution(mesh):
    sections, devices = mesh.devices.shape
    planes = devices // 2
    grid = Mesh(mesh.devices.reshape(sections, 2, planes), ("section", "side", "plane"))
    where = ("side", "plane")
    in_specs = (
        P(None, "section", where, None),
        P(),
        P(None, "section", where, None),
        P(None, "section", where, None),
        P(),
        P(where, None, None),
        P(where, None, None),
        P(where, None, None),
    )
    out_specs = P(None, "section", where, None)
    return jax.shard_map(body, mesh=grid, in_specs=in_specs, out_specs=out_specs, check_vma=False)
```

```python
import functools

import jax
import jax.numpy as jnp
from jax import lax
from jax.experimental import pallas as pl
from jax.experimental.pallas import tpu as pltpu
from jax.sharding import Mesh
from jax.sharding import PartitionSpec as P

EPSILON = 1e-06
MOST = 6
LANES = 128


def passed_along(x, axis, by):
    peers = lax.axis_size(axis)
    pairs = [(i, i + by) for i in range(peers) if 0 <= i + by < peers]
    return lax.ppermute(x, axis, pairs)


def normalize(rows, gain):
    values = rows.astype(jnp.float32)
    scale = lax.rsqrt(jnp.mean(values * values, axis=-1, keepdims=True) + EPSILON)
    return (values * scale * gain).astype(jnp.bfloat16)


def exclusive_rank(onehot):
    before = jnp.cumsum(onehot, axis=-2) - onehot
    return jnp.sum(before * onehot, axis=-1)


def expert_kernel(units, blocks, per_slot, rows_in, gathered, out, weights, hidden, sem):
    planes, _, k_rows, _ = gathered.shape
    total, width = rows_in.shape
    count = weights.shape[0]
    per_unit = count // units
    sections = planes // units

    def copy(index):
        return pltpu.make_async_copy(gathered.at[:, index], weights.at[index], sem.at[index])

    order = [u * per_unit + part * blocks + b for part in range(3) for u in range(units) for b in range(blocks)]
    for index in order:
        copy(index).start()

    step = total // 3
    for pair in range(0, units * blocks, 2):
        columns = [(c // blocks, c % blocks) for c in (pair, pair + 1)]
        at = [u * per_unit + b for u, b in columns]
        for index in at:
            copy(index).wait()
            copy(index + blocks).wait()

        def load(offset):
            return jnp.concatenate(
                [weights[index + offset].reshape(width, LANES) for index in at], axis=1
            )

        @pl.loop(0, total // step)
        def _(i):
            rows = pl.ds(pl.multiple_of(i * step, 16), step)
            x = rows_in[rows, :]
            gate = jnp.dot(x, load(0), preferred_element_type=jnp.float32)
            up = jnp.dot(x, load(blocks), preferred_element_type=jnp.float32)
            value = gate / (1.0 + jnp.exp(-gate)) * up
            row = lax.broadcasted_iota(jnp.int32, value.shape, 0) + i * step
            column = lax.broadcasted_iota(jnp.int32, value.shape, 1)
            row_unit = row // per_slot % units
            column_unit = jnp.where(column < LANES, columns[0][0], columns[1][0])
            value = jnp.where(row_unit == column_unit, value, 0.0)
            hidden[rows, pair * LANES : (pair + 2) * LANES] = value.astype(jnp.bfloat16)

    for u in range(units):
        for b in range(blocks):
            copy(u * per_unit + 2 * blocks + b).wait()
    for first in range(0, sections, 2):

        def down(b):
            parts = [
                weights[u * per_unit + 2 * blocks + i, a * sections + b]
                for u in range(units)
                for a in range(units)
                for i in range(blocks)
            ]
            return jnp.concatenate(parts, axis=0)

        w = jnp.concatenate([down(first), down(first + 1)], axis=1)
        out[:, first * LANES : (first + 2) * LANES] = jnp.dot(
            hidden[...], w, preferred_element_type=jnp.float32
        ).astype(jnp.bfloat16)


def run_experts(received, gathered, units, blocks, per_slot, ff):
    total, width = received.shape
    vmem = pl.BlockSpec(memory_space=pltpu.VMEM)
    count = gathered.shape[1]
    shape = (count, gathered.shape[0]) + gathered.shape[2:]
    return pl.pallas_call(
        functools.partial(expert_kernel, units, blocks, per_slot),
        out_shape=jax.ShapeDtypeStruct((total, width), jnp.bfloat16),
        in_specs=[vmem, pl.BlockSpec(memory_space=pl.ANY)],
        out_specs=vmem,
        scratch_shapes=[
            pltpu.VMEM(shape, jnp.bfloat16),
            pltpu.VMEM((total, ff), jnp.bfloat16),
            pltpu.SemaphoreType.DMA((count,)),
        ],
        cost_estimate=pl.CostEstimate(
            flops=6 * total * width * ff,
            bytes_accessed=2 * gathered.size + 4 * total * width,
            transcendentals=total * ff,
        ),
        compiler_params=pltpu.CompilerParams(vmem_limit_bytes=40 << 20),
    )(received, gathered)


def body(tokens, norm_gain, expert_ids, route_scores, placement, w_gate, w_up, w_down):
    sections = lax.axis_size("section")
    sides = lax.axis_size("side")
    planes = lax.axis_size("plane")
    section = lax.axis_index("section")
    side = lax.axis_index("side")
    plane = lax.axis_index("plane")
    slots = placement.shape[0]
    experts = slots * 3 // 8
    width = tokens.shape[3]
    ff = w_gate.shape[2]
    half_ff = ff // 2
    units = planes // sections
    tok_rows = tokens.shape[2]
    top = expert_ids.shape[3]
    micros = tokens.shape[0]

    expert_range = jnp.arange(experts, dtype=jnp.int32)
    owner = (placement[:, None] == expert_range[None, :]).astype(jnp.int32)
    slot_rank = exclusive_rank(owner)
    slot_range = jnp.arange(slots, dtype=jnp.int32)
    mine = slot_range == side * planes + plane
    half = jnp.sum(jnp.where(mine, slot_rank, 0)) % 2

    k_rows = width // planes
    f_rows = half_ff // units
    blocks = half_ff // LANES

    def piece(number):
        def columns(w):
            part = lax.dynamic_slice(
                w[0], (number * k_rows, half * half_ff), (k_rows, half_ff)
            )
            return part.reshape(k_rows, blocks, LANES).transpose(1, 0, 2)

        down = lax.dynamic_slice(
            w_down[0],
            (half * half_ff + number // sections * f_rows, number % sections * LANES),
            (f_rows, LANES),
        ).reshape(f_rows // k_rows, k_rows, LANES)
        return jnp.concatenate([columns(w_gate), columns(w_up), down], axis=0)

    def offset_of(q):
        return q // 2 if q % 2 == 0 else (sections - q // 2 if q > 1 else sections // 2)

    offsets = [offset_of(q) for q in range(sections)]
    pair = section // 2
    odd = jnp.where(pair == 0, sections // 2, sections - pair)
    offset = jnp.where(section % 2 == 0, pair, odd)
    arrived = []
    for i in range(units):
        number = (plane + offset + i * sections) % planes
        moves = [
            (q * planes + j, q * planes + (j + offsets[q] + i * sections) % planes)
            for q in range(sections)
            for j in range(planes)
        ]
        arrived.append(lax.ppermute(piece(number), ("section", "plane"), moves))
    moves = [
        (q * planes + m, (m - offsets[q]) % sections * planes + m)
        for q in range(sections)
        for m in range(planes)
    ]
    share = lax.ppermute(jnp.stack(arrived), ("section", "plane"), moves)
    first = (plane - (plane - section) % sections) % planes // sections
    share = jnp.concatenate(
        [
            functools.reduce(
                lambda x, i: jnp.where(first == i, share[(u - i) % units], x),
                range(1, units),
                share[u],
            )
            for u in range(units)
        ],
        axis=0,
    )
    gathered = lax.all_gather(share, "plane", axis=0)
    per_slot = micros * MOST
    per_host = units * per_slot
    slot_side = slot_range // planes
    slot_plane = slot_range % planes
    slot_base = (
        slot_plane % sections * sides + slot_side
    ) * per_host + slot_plane // sections * per_slot
    bases = [
        jnp.sum(jnp.where(slot_rank == h, slot_base, 0)[:, None] * owner, axis=0) for h in range(2)
    ]
    ids = expert_ids[:, 0].reshape(micros, tok_rows * top)
    hit = (ids[:, :, None] == expert_range).astype(jnp.int32)
    rank = exclusive_rank(hit) + MOST * jnp.arange(micros, dtype=jnp.int32)[:, None]
    scores = route_scores[:, 0]
    probs = scores / jnp.sum(scores, axis=-1, keepdims=True)
    total = sections * sides * per_host
    buffer_range = jnp.arange(total, dtype=jnp.int32)
    take = jnp.zeros((micros * tok_rows, total), jnp.float32)
    mixing = jnp.zeros((micros * tok_rows, total), jnp.float32)
    for base in bases:
        index = (jnp.sum(hit * base, axis=-1) + rank).reshape(micros * tok_rows, top)
        for k in range(top):
            at = index[:, k : k + 1] == buffer_range
            take = jnp.where(at, 1.0, take)
            mixing = jnp.where(at, probs[:, :, k].reshape(-1, 1), mixing)

    normed = normalize(tokens[:, 0].reshape(micros * tok_rows, width), norm_gain)
    send = lax.dot_general(
        take.astype(jnp.bfloat16),
        normed,
        (((0,), (0,)), ((), ())),
        preferred_element_type=jnp.float32,
    ).astype(jnp.bfloat16)
    hosts = sections * sides

    def exchange(x):
        x = x.reshape(hosts, per_host, width)
        x = lax.all_to_all(x, ("section", "side"), split_axis=0, concat_axis=0, tiled=True)
        return x.reshape(total, width)

    received = exchange(send)
    partial = run_experts(received, gathered, units, blocks, per_slot, ff)
    returned = exchange(partial)
    moe = jnp.dot(
        mixing,
        returned.astype(jnp.float32),
        precision=lax.Precision.HIGHEST,
        preferred_element_type=jnp.float32,
    )
    mixed = tokens[:, 0].astype(jnp.float32) + moe.reshape(micros, tok_rows, width)
    mixed = mixed.astype(jnp.bfloat16)
    forward = passed_along(mixed[0], "section", 1)
    backward = passed_along(mixed[1], "section", -1)
    return jnp.stack([forward, backward], axis=0)[:, None]


def solution(mesh):
    sections, devices = mesh.devices.shape
    planes = devices // 2
    grid = Mesh(mesh.devices.reshape(sections, 2, planes), ("section", "side", "plane"))
    where = ("side", "plane")
    in_specs = (
        P(None, "section", where, None),
        P(),
        P(None, "section", where, None),
        P(None, "section", where, None),
        P(),
        P(where, None, None),
        P(where, None, None),
        P(where, None, None),
    )
    out_specs = P(None, "section", where, None)
    return jax.shard_map(body, mesh=grid, in_specs=in_specs, out_specs=out_specs, check_vma=False)
```

```python
import functools

import jax
import jax.numpy as jnp
from jax import lax
from jax.experimental import pallas as pl
from jax.experimental.pallas import tpu as pltpu
from jax.sharding import Mesh
from jax.sharding import PartitionSpec as P

EPSILON = 1e-06
MOST = 6
LANES = 128


def passed_along(x, axis, by):
    peers = lax.axis_size(axis)
    pairs = [(i, i + by) for i in range(peers) if 0 <= i + by < peers]
    return lax.ppermute(x, axis, pairs)


def normalize(rows, gain):
    values = rows.astype(jnp.float32)
    scale = lax.rsqrt(jnp.mean(values * values, axis=-1, keepdims=True) + EPSILON)
    return (values * scale * gain).astype(jnp.bfloat16)


def exclusive_rank(onehot):
    before = jnp.cumsum(onehot, axis=-2) - onehot
    return jnp.sum(before * onehot, axis=-1)


def expert_kernel(units, blocks, per_slot, place, rows_in, gathered, out, weights, hidden, sems):
    planes = gathered.shape[0]
    k_rows = gathered.shape[3]
    total, width = rows_in.shape
    per_unit = gathered.shape[1]
    sections = planes // units

    def copies(part, u):
        home = place[0] + u * sections
        for r in range(sections):
            shift = lax.rem(r - home + planes + sections // 2, sections)
            m = lax.rem(home + planes - sections // 2 + shift, planes)
            yield pltpu.make_async_copy(
                gathered.at[m, pl.ds(part * blocks, blocks)],
                weights.at[pl.ds(u * per_unit + part * blocks, blocks), :, r],
                sems.at[part, u, r],
            )

    for part in range(3):
        for u in range(units):
            for copy in copies(part, u):
                copy.start()

    def arrive(part, u):
        for copy in copies(part, u):
            copy.wait()

    for part in range(2):
        for u in range(units):
            arrive(part, u)
    step = total // 3
    for pair in range(0, units * blocks, 2):
        columns = [(c // blocks, c % blocks) for c in (pair, pair + 1)]
        at = [u * per_unit + b for u, b in columns]

        def load(offset):
            return jnp.concatenate(
                [weights[index + offset].reshape(width, LANES) for index in at], axis=1
            )

        @pl.loop(0, total // step)
        def _(i):
            rows = pl.ds(pl.multiple_of(i * step, 16), step)
            x = rows_in[rows, :]
            gate = jnp.dot(x, load(0), preferred_element_type=jnp.float32)
            up = jnp.dot(x, load(blocks), preferred_element_type=jnp.float32)
            value = gate / (1.0 + jnp.exp(-gate)) * up
            row = lax.broadcasted_iota(jnp.int32, value.shape, 0) + i * step
            column = lax.broadcasted_iota(jnp.int32, value.shape, 1)
            row_unit = row // per_slot % units
            column_unit = jnp.where(column < LANES, columns[0][0], columns[1][0])
            value = jnp.where(row_unit == column_unit, value, 0.0)
            hidden[rows, pair * LANES : (pair + 2) * LANES] = value.astype(jnp.bfloat16)

    for u in range(units):
        arrive(2, u)
    for first in range(0, sections, 2):

        def down(b):
            parts = [
                weights[u * per_unit + 2 * blocks + i, a, b]
                for u in range(units)
                for a in range(2)
                for i in range(blocks)
            ]
            return jnp.concatenate(parts, axis=0)

        w = jnp.concatenate([down(first), down(first + 1)], axis=1)
        out[:, first * LANES : (first + 2) * LANES] = jnp.dot(
            hidden[...], w, preferred_element_type=jnp.float32
        ).astype(jnp.bfloat16)


def run_experts(received, gathered, place, units, blocks, per_slot, ff):
    total, width = received.shape
    vmem = pl.BlockSpec(memory_space=pltpu.VMEM)
    planes, per_unit, pieces, k_rows, lanes = gathered.shape
    shape = (units * per_unit, pieces, planes // units, k_rows, lanes)
    return pl.pallas_call(
        functools.partial(expert_kernel, units, blocks, per_slot),
        out_shape=jax.ShapeDtypeStruct((total, width), jnp.bfloat16),
        in_specs=[
            pl.BlockSpec(memory_space=pltpu.SMEM),
            vmem,
            pl.BlockSpec(memory_space=pl.ANY),
        ],
        out_specs=vmem,
        scratch_shapes=[
            pltpu.VMEM(shape, jnp.bfloat16),
            pltpu.VMEM((total, ff), jnp.bfloat16),
            pltpu.SemaphoreType.DMA((3, units, planes // units)),
        ],
        cost_estimate=pl.CostEstimate(
            flops=6 * total * width * ff,
            bytes_accessed=2 * gathered.size + 4 * total * width,
            transcendentals=total * ff,
        ),
        compiler_params=pltpu.CompilerParams(vmem_limit_bytes=40 << 20),
    )(place, received, gathered)


def body(tokens, norm_gain, expert_ids, route_scores, placement, w_gate, w_up, w_down):
    sections = lax.axis_size("section")
    sides = lax.axis_size("side")
    planes = lax.axis_size("plane")
    section = lax.axis_index("section")
    side = lax.axis_index("side")
    plane = lax.axis_index("plane")
    slots = placement.shape[0]
    experts = slots * 3 // 8
    width = tokens.shape[3]
    ff = w_gate.shape[2]
    half_ff = ff // 2
    units = planes // sections
    tok_rows = tokens.shape[2]
    top = expert_ids.shape[3]
    micros = tokens.shape[0]

    expert_range = jnp.arange(experts, dtype=jnp.int32)
    owner = (placement[:, None] == expert_range[None, :]).astype(jnp.int32)
    slot_rank = exclusive_rank(owner)
    slot_range = jnp.arange(slots, dtype=jnp.int32)
    mine = slot_range == side * planes + plane
    half = jnp.sum(jnp.where(mine, slot_rank, 0)) % 2

    k_rows = width // planes
    f_rows = half_ff // units
    blocks = half_ff // LANES

    def piece(number):
        def columns(w):
            part = lax.dynamic_slice(
                w[0], (number * k_rows, half * half_ff), (k_rows, half_ff)
            )
            return part.reshape(k_rows, blocks, LANES).transpose(1, 0, 2)

        down = lax.dynamic_slice(
            w_down[0],
            (half * half_ff + number // sections * f_rows, number % sections * LANES),
            (f_rows, LANES),
        ).reshape(f_rows // k_rows, k_rows, LANES)
        return jnp.concatenate([columns(w_gate), columns(w_up), down], axis=0)

    quarter = sections // 4

    def distance(q, i):
        step = q // 2 % quarter
        back = (step - sections // 2) if q % 2 == 0 else -1 - step
        ahead = (sections // 2 - 1 - step) if q % 2 == 0 else step
        return back if (q // 2 < quarter) == (i == 0) else ahead

    def my_distance(i):
        step = section // 2 % quarter
        even = section % 2 == 0
        back = jnp.where(even, step - sections // 2, -1 - step)
        ahead = jnp.where(even, sections // 2 - 1 - step, step)
        return jnp.where((section // 2 < quarter) == (i == 0), back, ahead)

    arrived = []
    for i in range(2):
        target = (plane + my_distance(i)) % planes
        number = i * sections + target % sections
        moves = [
            (q * planes + j, q * planes + (j + distance(q, i)) % planes)
            for q in range(sections)
            for j in range(planes)
        ]
        arrived.append(lax.ppermute(piece(number), ("section", "plane"), moves))
    for i in range(2):
        moves = [
            (q * planes + m, (m - distance(q, i)) % sections * planes + m)
            for q in range(sections)
            for m in range(planes)
        ]
        arrived[i] = lax.ppermute(arrived[i], ("section", "plane"), moves)
    share = jnp.stack(arrived, axis=1)

    routing = jnp.concatenate([expert_ids[:, 0].astype(jnp.float32), route_scores[:, 0]], axis=-1)
    share, tokens, routing = lax.optimization_barrier((share, tokens, routing))
    ways = (1, -1)
    tokens = jnp.stack([passed_along(tokens[m, 0], "section", ways[m]) for m in range(micros)])
    routing = jnp.stack([passed_along(routing[m], "section", ways[m]) for m in range(micros)])
    filled = jnp.stack([section > 0, section < sections - 1])
    expert_ids = routing[:, :, :top].astype(jnp.int32)
    scores = routing[:, :, top:]
    gathered = lax.all_gather(share, "plane", axis=0)
    per_slot = micros * MOST
    per_host = units * per_slot
    slot_side = slot_range // planes
    slot_plane = slot_range % planes
    slot_base = (
        slot_plane % sections * sides + slot_side
    ) * per_host + slot_plane // sections * per_slot
    bases = [
        jnp.sum(jnp.where(slot_rank == h, slot_base, 0)[:, None] * owner, axis=0) for h in range(2)
    ]
    ids = expert_ids.reshape(micros, tok_rows * top)
    hit = (ids[:, :, None] == expert_range).astype(jnp.int32)
    rank = exclusive_rank(hit) + MOST * jnp.arange(micros, dtype=jnp.int32)[:, None]
    probs = scores / jnp.sum(scores, axis=-1, keepdims=True)
    probs = jnp.where(filled[:, None, None], probs, 0.0)
    total = sections * sides * per_host
    buffer_range = jnp.arange(total, dtype=jnp.int32)
    take = jnp.zeros((micros * tok_rows, total), jnp.float32)
    mixing = jnp.zeros((micros * tok_rows, total), jnp.float32)
    for base in bases:
        index = (jnp.sum(hit * base, axis=-1) + rank).reshape(micros * tok_rows, top)
        for k in range(top):
            at = index[:, k : k + 1] == buffer_range
            take = jnp.where(at, 1.0, take)
            mixing = jnp.where(at, probs[:, :, k].reshape(-1, 1), mixing)

    normed = normalize(tokens.reshape(micros * tok_rows, width), norm_gain)
    send = lax.dot_general(
        take.astype(jnp.bfloat16),
        normed,
        (((0,), (0,)), ((), ())),
        preferred_element_type=jnp.float32,
    ).astype(jnp.bfloat16)
    hosts = sections * sides

    def exchange(x):
        x = x.reshape(hosts, per_host, width)
        x = lax.all_to_all(x, ("section", "side"), split_axis=0, concat_axis=0, tiled=True)
        return x.reshape(total, width)

    received = exchange(send)
    place = jnp.full((1,), section, jnp.int32)
    partial = run_experts(received, gathered, place, units, blocks, per_slot, ff)
    returned = exchange(partial)
    moe = jnp.dot(
        mixing,
        returned.astype(jnp.float32),
        precision=lax.Precision.HIGHEST,
        preferred_element_type=jnp.float32,
    )
    mixed = tokens.astype(jnp.float32) + moe.reshape(micros, tok_rows, width)
    mixed = jnp.where(filled[:, None, None], mixed, 0.0)
    return mixed.astype(jnp.bfloat16)[:, None]


def solution(mesh):
    sections, devices = mesh.devices.shape
    planes = devices // 2
    grid = Mesh(mesh.devices.reshape(sections, 2, planes), ("section", "side", "plane"))
    where = ("side", "plane")
    in_specs = (
        P(None, "section", where, None),
        P(),
        P(None, "section", where, None),
        P(None, "section", where, None),
        P(),
        P(where, None, None),
        P(where, None, None),
        P(where, None, None),
    )
    out_specs = P(None, "section", where, None)
    return jax.shard_map(body, mesh=grid, in_specs=in_specs, out_specs=out_specs, check_vma=False)
```

```python
import functools

import jax
import jax.numpy as jnp
from jax import lax
from jax.experimental import pallas as pl
from jax.experimental.pallas import tpu as pltpu
from jax.sharding import Mesh
from jax.sharding import PartitionSpec as P

EPSILON = 1e-06
MOST = 6
LANES = 128


def passed_along(x, axis, by):
    peers = lax.axis_size(axis)
    pairs = [(i, i + by) for i in range(peers) if 0 <= i + by < peers]
    return lax.ppermute(x, axis, pairs)


def normalize(rows, gain):
    values = rows.astype(jnp.float32)
    scale = lax.rsqrt(jnp.mean(values * values, axis=-1, keepdims=True) + EPSILON)
    return (values * scale * gain).astype(jnp.bfloat16)


def exclusive_rank(onehot):
    before = jnp.cumsum(onehot, axis=-2) - onehot
    return jnp.sum(before * onehot, axis=-1)


def expert_kernel(units, blocks, per_slot, stretch, place, rows_in, gathered, out, weights, hidden, sems):
    planes = gathered.shape[0]
    k_rows = gathered.shape[3]
    width = rows_in.shape[2]
    per_unit = gathered.shape[1]
    sections = planes // units

    def copies(part, u):
        home = place[0] + u * sections
        for r in range(sections):
            shift = lax.rem(r - home + planes + sections // 2, sections)
            m = lax.rem(home + planes - sections // 2 + shift, planes)
            yield pltpu.make_async_copy(
                gathered.at[m, pl.ds(part * blocks, blocks)],
                weights.at[pl.ds(u * per_unit + part * blocks, blocks), :, r],
                sems.at[part, u, r],
            )

    for u in range(units):
        for part in range(2):
            for copy in copies(part, u):
                copy.start()
    for u in range(units):
        for copy in copies(2, u):
            copy.start()

    def arrive(part, u):
        for copy in copies(part, u):
            copy.wait()

    sources = rows_in.shape[0]
    spare = stretch - per_slot
    step = sources // 2
    for u in range(units):
        arrive(0, u)
        arrive(1, u)

        def load(*columns):
            return jnp.concatenate(
                [weights[u * per_unit + c].reshape(width, LANES) for c in columns], axis=1
            )

        @pl.loop(0, sources // step)
        def _(i):
            at = pl.ds(i * step, step)
            x = rows_in[at, u * (2 * per_slot - stretch) : u * (2 * per_slot - stretch) + stretch, :]
            x = x.reshape(step * stretch, width)

            def product(*columns):
                return jnp.dot(x, load(*columns), preferred_element_type=jnp.float32)

            row = lax.broadcasted_iota(jnp.int32, (step * stretch, LANES), 0)
            row = lax.rem(row, stretch)
            own = row < per_slot if u == 0 else row >= spare
            gate_two = product(0, 1)
            up_two = product(blocks, blocks + 1)
            both = product(2, blocks + 2)
            parts = [
                (gate_two[:, :LANES], up_two[:, :LANES]),
                (gate_two[:, LANES:], up_two[:, LANES:]),
                (both[:, :LANES], both[:, LANES:]),
            ]
            out_rows = pl.ds(pl.multiple_of(i * (step * stretch), step * stretch), step * stretch)
            for b, (gate, up) in enumerate(parts):
                value = gate / (1.0 + jnp.exp(-gate)) * up
                value = jnp.where(own, value, 0.0).astype(jnp.bfloat16)
                hidden[u, out_rows, b * LANES : (b + 1) * LANES] = value

    for u in range(units):
        arrive(2, u)
    edge = 2 * per_slot - stretch
    for first in range(0, sections, 2):

        def down(u, b):
            parts = [
                weights[u * per_unit + 2 * blocks + i, a, b] for a in range(2) for i in range(blocks)
            ]
            return jnp.concatenate(parts, axis=0)

        y = []
        for u in range(units):
            w = jnp.concatenate([down(u, first), down(u, first + 1)], axis=1)
            y.append(
                jnp.dot(hidden[u], w, preferred_element_type=jnp.float32).reshape(
                    sources, stretch, 2 * LANES
                )
            )
        joined = jnp.concatenate(
            [y[0][:, :edge], y[0][:, edge:] + y[1][:, : stretch - edge], y[1][:, stretch - edge :]],
            axis=1,
        )
        out[:, :, first * LANES : (first + 2) * LANES] = joined.astype(jnp.bfloat16)


def run_experts(received, gathered, place, units, blocks, per_slot, ff):
    sources, per_host, width = received.shape
    total = sources * per_host
    stretch = -(-per_slot // 8) * 8
    vmem = pl.BlockSpec(memory_space=pltpu.VMEM)
    planes, per_unit, pieces, k_rows, lanes = gathered.shape
    shape = (units * per_unit, pieces, planes // units, k_rows, lanes)
    return pl.pallas_call(
        functools.partial(expert_kernel, units, blocks, per_slot, stretch),
        out_shape=jax.ShapeDtypeStruct(received.shape, jnp.bfloat16),
        in_specs=[
            pl.BlockSpec(memory_space=pltpu.SMEM),
            vmem,
            pl.BlockSpec(memory_space=pl.ANY),
        ],
        out_specs=vmem,
        scratch_shapes=[
            pltpu.VMEM(shape, jnp.bfloat16),
            pltpu.VMEM((units, sources * stretch, ff // units), jnp.bfloat16),
            pltpu.SemaphoreType.DMA((3, units, planes // units)),
        ],
        cost_estimate=pl.CostEstimate(
            flops=6 * total * width * ff,
            bytes_accessed=2 * gathered.size + 4 * total * width,
            transcendentals=total * ff,
        ),
        compiler_params=pltpu.CompilerParams(vmem_limit_bytes=40 << 20),
    )(place, received, gathered)


def body(tokens, norm_gain, expert_ids, route_scores, placement, w_gate, w_up, w_down):
    sections = lax.axis_size("section")
    sides = lax.axis_size("side")
    planes = lax.axis_size("plane")
    section = lax.axis_index("section")
    side = lax.axis_index("side")
    plane = lax.axis_index("plane")
    slots = placement.shape[0]
    experts = slots * 3 // 8
    width = tokens.shape[3]
    ff = w_gate.shape[2]
    half_ff = ff // 2
    units = planes // sections
    tok_rows = tokens.shape[2]
    top = expert_ids.shape[3]
    micros = tokens.shape[0]

    slot_range = jnp.arange(slots, dtype=jnp.int32)
    mine = side * planes + plane
    my_expert = jnp.sum(jnp.where(slot_range == mine, placement, 0))
    half = jnp.sum(((placement == my_expert) & (slot_range < mine)).astype(jnp.int32)) % 2

    k_rows = width // planes
    f_rows = half_ff // units
    blocks = half_ff // LANES

    def piece(number):
        def columns(w):
            part = lax.dynamic_slice(
                w[0], (number * k_rows, half * half_ff), (k_rows, half_ff)
            )
            return [part[:, b * LANES : (b + 1) * LANES] for b in range(blocks)]

        down = lax.dynamic_slice(
            w_down[0],
            (half * half_ff + number // sections * f_rows, number % sections * LANES),
            (f_rows, LANES),
        )
        return jnp.concatenate([*columns(w_gate), *columns(w_up), down], axis=0)

    quarter = sections // 4

    def distance(q, i):
        step = q // 2 % quarter
        back = (step - sections // 2) if q % 2 == 0 else -1 - step
        ahead = (sections // 2 - 1 - step) if q % 2 == 0 else step
        return back if (q // 2 < quarter) == (i == 0) else ahead

    def my_distance(i):
        step = section // 2 % quarter
        even = section % 2 == 0
        back = jnp.where(even, step - sections // 2, -1 - step)
        ahead = jnp.where(even, sections // 2 - 1 - step, step)
        return jnp.where((section // 2 < quarter) == (i == 0), back, ahead)

    arrived = []
    for i in range(2):
        target = (plane + my_distance(i)) % planes
        number = i * sections + target % sections
        moves = [
            (q * planes + j, q * planes + (j + distance(q, i)) % planes)
            for q in range(sections)
            for j in range(planes)
        ]
        arrived.append(lax.ppermute(piece(number), ("section", "plane"), moves))
    for i in range(2):
        moves = [
            (q * planes + m, (m - distance(q, i)) % sections * planes + m)
            for q in range(sections)
            for m in range(planes)
        ]
        arrived[i] = lax.ppermute(arrived[i], ("section", "plane"), moves)
    share = jnp.stack([x.reshape(-1, k_rows, LANES) for x in arrived], axis=1)
    share = share.reshape(-1, LANES)

    routing = jnp.concatenate([expert_ids[:, 0].astype(jnp.float32), route_scores[:, 0]], axis=-1)
    share, tokens, routing, placement = lax.optimization_barrier(
        (share, tokens, routing, placement)
    )
    expert_range = jnp.arange(experts, dtype=jnp.int32)
    owner = (placement[:, None] == expert_range[None, :]).astype(jnp.int32)
    slot_rank = exclusive_rank(owner)
    ways = (1, -1)
    tokens = jnp.stack([passed_along(tokens[m, 0], "section", ways[m]) for m in range(micros)])
    routing = jnp.stack([passed_along(routing[m], "section", ways[m]) for m in range(micros)])
    filled = jnp.stack([section > 0, section < sections - 1])
    expert_ids = routing[:, :, :top].astype(jnp.int32)
    scores = routing[:, :, top:]
    gathered = lax.all_gather(share, "plane", axis=0)
    gathered = gathered.reshape(planes, -1, 2, k_rows, LANES)
    per_slot = micros * MOST
    per_host = units * per_slot
    slot_side = slot_range // planes
    slot_plane = slot_range % planes
    slot_base = (
        slot_plane % sections * sides + slot_side
    ) * per_host + slot_plane // sections * per_slot
    bases = [
        jnp.sum(jnp.where(slot_rank == h, slot_base, 0)[:, None] * owner, axis=0) for h in range(2)
    ]
    ids = expert_ids.reshape(micros, tok_rows * top)
    hit = (ids[:, :, None] == expert_range).astype(jnp.int32)
    rank = exclusive_rank(hit) + MOST * jnp.arange(micros, dtype=jnp.int32)[:, None]
    probs = scores / jnp.sum(scores, axis=-1, keepdims=True)
    probs = jnp.where(filled[:, None, None], probs, 0.0)
    total = sections * sides * per_host
    buffer_range = jnp.arange(total, dtype=jnp.int32)
    take = jnp.zeros((micros * tok_rows, total), jnp.float32)
    mixing = jnp.zeros((micros * tok_rows, total), jnp.float32)
    for base in bases:
        index = (jnp.sum(hit * base, axis=-1) + rank).reshape(micros * tok_rows, top)
        for k in range(top):
            at = index[:, k : k + 1] == buffer_range
            take = jnp.where(at, 1.0, take)
            mixing = jnp.where(at, probs[:, :, k].reshape(-1, 1), mixing)

    normed = normalize(tokens.reshape(micros * tok_rows, width), norm_gain)
    send = lax.dot_general(
        take.astype(jnp.bfloat16),
        normed,
        (((0,), (0,)), ((), ())),
        preferred_element_type=jnp.float32,
    ).astype(jnp.bfloat16)
    hosts = sections * sides

    def exchange(x):
        x = x.reshape(hosts, per_host, width)
        return lax.all_to_all(x, ("section", "side"), split_axis=0, concat_axis=0, tiled=True)

    received = exchange(send)
    place = jnp.full((1,), section, jnp.int32)
    partial = run_experts(received, gathered, place, units, blocks, per_slot, ff)
    returned = exchange(partial).reshape(total, width)
    moe = jnp.dot(
        mixing,
        returned.astype(jnp.float32),
        precision=lax.Precision.HIGH,
        preferred_element_type=jnp.float32,
    )
    mixed = tokens.astype(jnp.float32) + moe.reshape(micros, tok_rows, width)
    mixed = jnp.where(filled[:, None, None], mixed, 0.0)
    return mixed.astype(jnp.bfloat16)[:, None]


def solution(mesh):
    sections, devices = mesh.devices.shape
    planes = devices // 2
    grid = Mesh(mesh.devices.reshape(sections, 2, planes), ("section", "side", "plane"))
    where = ("side", "plane")
    in_specs = (
        P(None, "section", where, None),
        P(),
        P(None, "section", where, None),
        P(None, "section", where, None),
        P(),
        P(where, None, None),
        P(where, None, None),
        P(where, None, None),
    )
    out_specs = P(None, "section", where, None)
    return jax.shard_map(body, mesh=grid, in_specs=in_specs, out_specs=out_specs, check_vma=False)
```

```python
import functools

import jax
import jax.numpy as jnp
from jax import lax
from jax.experimental import pallas as pl
from jax.experimental.pallas import tpu as pltpu
from jax.sharding import Mesh
from jax.sharding import PartitionSpec as P

EPSILON = 1e-06
MOST = 6
LANES = 128


def passed_along(x, axis, by):
    peers = lax.axis_size(axis)
    pairs = [(i, i + by) for i in range(peers) if 0 <= i + by < peers]
    return lax.ppermute(x, axis, pairs)


def normalize(rows, gain):
    values = rows.astype(jnp.float32)
    scale = lax.rsqrt(jnp.mean(values * values, axis=-1, keepdims=True) + EPSILON)
    return (values * scale * gain).astype(jnp.bfloat16)


def exclusive_rank(onehot):
    before = jnp.cumsum(onehot, axis=-2) - onehot
    return jnp.sum(before * onehot, axis=-1)


def expert_kernel(units, blocks, per_slot, stretch, place, rows_in, gathered, out, weights, hidden, sems):
    planes = gathered.shape[0]
    k_rows = gathered.shape[3]
    width = rows_in.shape[2]
    per_unit = gathered.shape[1]
    sections = planes // units

    def copies(part, u):
        home = place[0] + u * sections
        for r in range(sections):
            shift = lax.rem(r - home + planes + sections // 2, sections)
            m = lax.rem(home + planes - sections // 2 + shift, planes)
            yield pltpu.make_async_copy(
                gathered.at[m, pl.ds(part * blocks, blocks)],
                weights.at[pl.ds(u * per_unit + part * blocks, blocks), :, r],
                sems.at[part, u, r],
            )

    for u in range(units):
        for part in range(2):
            for copy in copies(part, u):
                copy.start()
    for u in range(units):
        for copy in copies(2, u):
            copy.start()

    def arrive(part, u):
        for copy in copies(part, u):
            copy.wait()

    sources = rows_in.shape[0]
    spare = stretch - per_slot
    step = sources // 2
    for u in range(units):
        arrive(0, u)
        arrive(1, u)

        def load(*columns):
            return jnp.concatenate(
                [weights[u * per_unit + c].reshape(width, LANES) for c in columns], axis=1
            )

        @pl.loop(0, sources // step)
        def _(i):
            at = pl.ds(i * step, step)
            x = rows_in[at, u * (2 * per_slot - stretch) : u * (2 * per_slot - stretch) + stretch, :]
            x = x.reshape(step * stretch, width)

            def product(*columns):
                return jnp.dot(x, load(*columns), preferred_element_type=jnp.float32)

            row = lax.broadcasted_iota(jnp.int32, (step * stretch, LANES), 0)
            row = lax.rem(row, stretch)
            own = row < per_slot if u == 0 else row >= spare
            gate_two = product(0, 1)
            up_two = product(blocks, blocks + 1)
            both = product(2, blocks + 2)
            parts = [
                (gate_two[:, :LANES], up_two[:, :LANES]),
                (gate_two[:, LANES:], up_two[:, LANES:]),
                (both[:, :LANES], both[:, LANES:]),
            ]
            out_rows = pl.ds(pl.multiple_of(i * (step * stretch), step * stretch), step * stretch)
            for b, (gate, up) in enumerate(parts):
                value = gate / (1.0 + jnp.exp(-gate)) * up
                value = jnp.where(own, value, 0.0).astype(jnp.bfloat16)
                hidden[u, out_rows, b * LANES : (b + 1) * LANES] = value

    for u in range(units):
        arrive(2, u)
    edge = 2 * per_slot - stretch
    for first in range(0, sections, 2):

        def down(u, b):
            parts = [
                weights[u * per_unit + 2 * blocks + i, a, b] for a in range(2) for i in range(blocks)
            ]
            return jnp.concatenate(parts, axis=0)

        y = []
        for u in range(units):
            w = jnp.concatenate([down(u, first), down(u, first + 1)], axis=1)
            y.append(
                jnp.dot(hidden[u], w, preferred_element_type=jnp.float32).reshape(
                    sources, stretch, 2 * LANES
                )
            )
        joined = jnp.concatenate(
            [y[0][:, :edge], y[0][:, edge:] + y[1][:, : stretch - edge], y[1][:, stretch - edge :]],
            axis=1,
        )
        out[:, :, first * LANES : (first + 2) * LANES] = joined.astype(jnp.bfloat16)


def run_experts(received, gathered, place, units, blocks, per_slot, ff):
    sources, per_host, width = received.shape
    total = sources * per_host
    stretch = -(-per_slot // 8) * 8
    vmem = pl.BlockSpec(memory_space=pltpu.VMEM)
    planes, per_unit, pieces, k_rows, lanes = gathered.shape
    shape = (units * per_unit, pieces, planes // units, k_rows, lanes)
    return pl.pallas_call(
        functools.partial(expert_kernel, units, blocks, per_slot, stretch),
        out_shape=jax.ShapeDtypeStruct(received.shape, jnp.bfloat16),
        in_specs=[
            pl.BlockSpec(memory_space=pltpu.SMEM),
            vmem,
            pl.BlockSpec(memory_space=pl.ANY),
        ],
        out_specs=vmem,
        scratch_shapes=[
            pltpu.VMEM(shape, jnp.bfloat16),
            pltpu.VMEM((units, sources * stretch, ff // units), jnp.bfloat16),
            pltpu.SemaphoreType.DMA((3, units, planes // units)),
        ],
        cost_estimate=pl.CostEstimate(
            flops=6 * total * width * ff,
            bytes_accessed=2 * gathered.size + 4 * total * width,
            transcendentals=total * ff,
        ),
        compiler_params=pltpu.CompilerParams(vmem_limit_bytes=40 << 20),
    )(place, received, gathered)


def piece_kernel(sections, planes, k_rows, half_ff, placement, w_gate, w_up, w_down, *rest):
    *outs, sems = rest
    section = lax.axis_index("section")
    plane = lax.axis_index("plane")
    mine = lax.axis_index("side") * planes + plane
    blocks = half_ff // LANES
    f_rows = half_ff // 2
    my_expert = placement[mine]

    def count(s, total):
        return total + jnp.where((placement[s] == my_expert) & (s < mine), 1, 0)

    half = lax.rem(lax.fori_loop(0, placement.shape[0], count, 0, unroll=8), 2)
    quarter = sections // 4
    step = lax.rem(lax.div(section, 2), quarter)
    even = lax.rem(section, 2) == 0
    back = jnp.where(even, step - sections // 2, -1 - step)
    ahead = jnp.where(even, sections // 2 - 1 - step, step)
    copies = []
    for i, out in enumerate(outs):
        distance = jnp.where((lax.div(section, 2) < quarter) == (i == 0), back, ahead)
        place = lax.rem(plane + distance + planes, sections)
        rows = pl.ds(pl.multiple_of((i * sections + place) * k_rows, k_rows), k_rows)
        parts = []
        for w in (w_gate, w_up):
            for b in range(blocks):
                columns = pl.ds(pl.multiple_of(half * half_ff + b * LANES, LANES), LANES)
                parts.append((w.at[0, rows, columns], k_rows))
        rows = pl.ds(pl.multiple_of(half * half_ff + i * f_rows, k_rows), f_rows)
        parts.append((w_down.at[0, rows, pl.ds(pl.multiple_of(place * LANES, LANES), LANES)], f_rows))
        first = 0
        for part, length in parts:
            copies.append(
                pltpu.make_async_copy(part, out.at[pl.ds(first, length)], sems.at[len(copies)])
            )
            first += length
    for copy in copies:
        copy.start()
    for copy in copies:
        copy.wait()


def cut_pieces(placement, w_gate, w_up, w_down, sections, planes):
    width, ff = w_gate.shape[1:]
    half_ff = ff // 2
    k_rows = width // planes
    lines = 2 * (half_ff // LANES) * k_rows + half_ff // 2
    shape = jax.ShapeDtypeStruct((lines, LANES), w_gate.dtype)
    vmem = pl.BlockSpec(memory_space=pltpu.VMEM)
    hbm = pl.BlockSpec(memory_space=pl.ANY)
    return pl.pallas_call(
        functools.partial(piece_kernel, sections, planes, k_rows, half_ff),
        out_shape=(shape, shape),
        in_specs=[pl.BlockSpec(memory_space=pltpu.SMEM), hbm, hbm, hbm],
        out_specs=(vmem, vmem),
        scratch_shapes=[pltpu.SemaphoreType.DMA((2 * (2 * (half_ff // LANES) + 1),))],
        cost_estimate=pl.CostEstimate(
            flops=0, bytes_accessed=8 * lines * LANES, transcendentals=0
        ),
    )(placement, w_gate, w_up, w_down)


def body(tokens, norm_gain, expert_ids, route_scores, placement, w_gate, w_up, w_down):
    sections = lax.axis_size("section")
    sides = lax.axis_size("side")
    planes = lax.axis_size("plane")
    section = lax.axis_index("section")
    side = lax.axis_index("side")
    plane = lax.axis_index("plane")
    slots = placement.shape[0]
    experts = slots * 3 // 8
    width = tokens.shape[3]
    ff = w_gate.shape[2]
    half_ff = ff // 2
    units = planes // sections
    tok_rows = tokens.shape[2]
    top = expert_ids.shape[3]
    micros = tokens.shape[0]

    expert_range = jnp.arange(experts, dtype=jnp.int32)
    slot_range = jnp.arange(slots, dtype=jnp.int32)
    k_rows = width // planes
    blocks = half_ff // LANES

    quarter = sections // 4

    def distance(q, i):
        step = q // 2 % quarter
        back = (step - sections // 2) if q % 2 == 0 else -1 - step
        ahead = (sections // 2 - 1 - step) if q % 2 == 0 else step
        return back if (q // 2 < quarter) == (i == 0) else ahead

    pieces = cut_pieces(placement, w_gate, w_up, w_down, sections, planes)
    arrived = []
    for i in range(2):
        moves = [
            (q * planes + j, q * planes + (j + distance(q, i)) % planes)
            for q in range(sections)
            for j in range(planes)
        ]
        arrived.append(lax.ppermute(pieces[i], ("section", "plane"), moves))
    for i in range(2):
        moves = [
            (q * planes + m, (m - distance(q, i)) % sections * planes + m)
            for q in range(sections)
            for m in range(planes)
        ]
        arrived[i] = lax.ppermute(arrived[i], ("section", "plane"), moves)
    share = jnp.stack([x.reshape(-1, k_rows, LANES) for x in arrived], axis=1)
    share = share.reshape(-1, LANES)

    routing = jnp.concatenate([expert_ids[:, 0].astype(jnp.float32), route_scores[:, 0]], axis=-1)
    share, tokens, routing, placement = lax.optimization_barrier(
        (share, tokens, routing, placement)
    )
    owner = (placement[:, None] == expert_range[None, :]).astype(jnp.int32)
    slot_rank = exclusive_rank(owner)
    ways = (1, -1)
    tokens = jnp.stack([passed_along(tokens[m, 0], "section", ways[m]) for m in range(micros)])
    routing = jnp.stack([passed_along(routing[m], "section", ways[m]) for m in range(micros)])
    filled = jnp.stack([section > 0, section < sections - 1])
    expert_ids = routing[:, :, :top].astype(jnp.int32)
    scores = routing[:, :, top:]
    gathered = lax.all_gather(share, "plane", axis=0)
    gathered = gathered.reshape(planes, -1, 2, k_rows, LANES)
    per_slot = micros * MOST
    per_host = units * per_slot
    slot_side = slot_range // planes
    slot_plane = slot_range % planes
    slot_base = (
        slot_plane % sections * sides + slot_side
    ) * per_host + slot_plane // sections * per_slot
    bases = [
        jnp.sum(jnp.where(slot_rank == h, slot_base, 0)[:, None] * owner, axis=0) for h in range(2)
    ]
    ids = expert_ids.reshape(micros, tok_rows * top)
    hit = (ids[:, :, None] == expert_range).astype(jnp.int32)
    rank = exclusive_rank(hit) + MOST * jnp.arange(micros, dtype=jnp.int32)[:, None]
    probs = scores / jnp.sum(scores, axis=-1, keepdims=True)
    probs = jnp.where(filled[:, None, None], probs, 0.0)
    total = sections * sides * per_host
    buffer_range = jnp.arange(total, dtype=jnp.int32)
    take = jnp.zeros((micros * tok_rows, total), jnp.float32)
    mixing = jnp.zeros((micros * tok_rows, total), jnp.float32)
    for base in bases:
        index = (jnp.sum(hit * base, axis=-1) + rank).reshape(micros * tok_rows, top)
        for k in range(top):
            at = index[:, k : k + 1] == buffer_range
            take = jnp.where(at, 1.0, take)
            mixing = jnp.where(at, probs[:, :, k].reshape(-1, 1), mixing)

    normed = normalize(tokens.reshape(micros * tok_rows, width), norm_gain)
    send = lax.dot_general(
        take.astype(jnp.bfloat16),
        normed,
        (((0,), (0,)), ((), ())),
        preferred_element_type=jnp.float32,
    ).astype(jnp.bfloat16)
    hosts = sections * sides

    def exchange(x):
        x = x.reshape(hosts, per_host, width)
        return lax.all_to_all(x, ("section", "side"), split_axis=0, concat_axis=0, tiled=True)

    received = exchange(send)
    place = jnp.full((1,), section, jnp.int32)
    partial = run_experts(received, gathered, place, units, blocks, per_slot, ff)
    returned = exchange(partial).reshape(total, width)
    moe = jnp.dot(
        mixing,
        returned.astype(jnp.float32),
        precision=lax.Precision.HIGH,
        preferred_element_type=jnp.float32,
    )
    mixed = tokens.astype(jnp.float32) + moe.reshape(micros, tok_rows, width)
    mixed = jnp.where(filled[:, None, None], mixed, 0.0)
    return mixed.astype(jnp.bfloat16)[:, None]


def solution(mesh):
    sections, devices = mesh.devices.shape
    planes = devices // 2
    grid = Mesh(mesh.devices.reshape(sections, 2, planes), ("section", "side", "plane"))
    where = ("side", "plane")
    in_specs = (
        P(None, "section", where, None),
        P(),
        P(None, "section", where, None),
        P(None, "section", where, None),
        P(),
        P(where, None, None),
        P(where, None, None),
        P(where, None, None),
    )
    out_specs = P(None, "section", where, None)
    return jax.shard_map(body, mesh=grid, in_specs=in_specs, out_specs=out_specs, check_vma=False)
```
